32 devices in a mesh: row: 8 (over y, x, core), col: 4 (over z).
Axes of the slice: x: 2, y: 2, z: 4, core: 2. Of those that a mesh axis runs over, the one named last changes fastest.
Arguments:
- matrix: bfloat16 [3072, 3072], P('row', 'col'), may hold values from 3.2484531e-06 to 0.0012969971
- occ_matrix: int32 [24, 24], P('row', 'col'), may hold values 0 or 1
- batch: bfloat16 [3072, 512], P('row', 'col'), may hold values from 0.0099487305 to 4
- occ_batch: int32 [24, 4], P('row', 'col'), may hold values 0 or 1
- prune_mask: int32 [3072, 512], P('row', 'col'), may hold values 0 or 1
Outputs:
- clustered: float32 [3072, 512], P('row', 'col')
The draws below stay inside these ranges and needn't reach their ends.
All inputs are finite; a program needn't handle non-finite values. No bound on the sum of `occ_matrix` or of `occ_batch` or of `prune_mask` on one device may be relied on, other than what follows from the above.
Results may differ from the reference program's by a relative error of at most 0.0003.
Values may be sent and summed in bfloat16 or wider, within the bound.
A program may use at most 64 MiB of HBM per device.

```python
import math
import jax
import jax.numpy as jnp

TILE = 128
N = 3072
NB = 512


def touch_ends(result, own_key, low, high):
    extent = result.shape
    index_at = [jax.random.randint(jax.random.fold_in(own_key, axis), (), 0, extent[axis]) for axis in range(len(extent))]
    result = result.at[tuple(index_at)].set(low)
    longest = extent.index(max(extent))
    index_at[longest] = (index_at[longest] + 1) % extent[longest]
    return result.at[tuple(index_at)].set(high)


def steps_of(key, dims, shards, low, top_value):
    factor_of, own = 1.0, jax.random.fold_in(key, 6)
    for position, shards_of in shards:
        draws = jnp.exp(jax.random.uniform(jax.random.fold_in(own, position), (shards_of,), jnp.float32, low / len(shards), top_value / len(shards)))
        factor_of = factor_of * jnp.repeat(draws, dims[position] // shards_of).reshape([-1 if axis == position else 1 for axis in range(len(dims))])
    return factor_of


def setup_inputs(seed: int = 0) -> dict:
    key_list = jax.random.split(jax.random.key(seed), 6)
    return {
        "matrix": jnp.clip(jnp.exp(math.log(0.0012969971) - 5.989628 * jax.random.uniform(key_list[0], (N, N), jnp.float32) ** steps_of(key_list[0], (N, N), ((0, 8), (1, 4)), -0.2, 0.2)), 3.248453140258789e-06, 0.0012969971).astype(jnp.bfloat16),
        "occ_matrix": touch_ends((jax.random.randint(key_list[1], (N // TILE, N // TILE), 0, 4) < 3).astype(jnp.int32), jax.random.fold_in(key_list[1], 1), 0, 1),
        "batch": jnp.clip(jnp.exp(math.log(4.0) - 5.996605 * jax.random.uniform(key_list[2], (N, NB), jnp.float32) ** steps_of(key_list[2], (N, NB), ((0, 8), (1, 4)), -0.2, 0.2)), 0.0099487305, 4.0).astype(jnp.bfloat16),
        "occ_batch": touch_ends((jax.random.randint(key_list[3], (N // TILE, NB // TILE), 0, 4) < 3).astype(jnp.int32), jax.random.fold_in(key_list[3], 1), 0, 1),
        "prune_mask": touch_ends((jax.random.randint(key_list[4], (N, NB), 0, 8) < 7).astype(jnp.int32), jax.random.fold_in(key_list[4], 1), 0, 1),
    }


def expand_tiles(occupancy, size):
    return jnp.repeat(jnp.repeat(occupancy, size, axis=0), size, axis=1)


def reference(matrix, occ_matrix, batch, occ_batch, prune_mask):
    stored_matrix = matrix * expand_tiles(occ_matrix, TILE).astype(jnp.bfloat16)
    stored_batch = batch * expand_tiles(occ_batch, TILE).astype(jnp.bfloat16)
    expanded = jnp.dot(stored_matrix, stored_batch, preferred_element_type=jnp.float32)
    kept = expanded * prune_mask.astype(jnp.float32)
    inflated = kept * kept
    col_total = jnp.sum(inflated, axis=0)
    return inflated / (col_total[None, :] / N + 1e-5)
```

```python
import functools

import jax
import jax.numpy as jnp
from jax import lax
from jax.experimental import pallas as pl
from jax.experimental.pallas import tpu as pltpu
from jax.sharding import PartitionSpec as P

MESH = pl.DeviceIdType.MESH


def expand_tiles(occupancy, size):
    return jnp.repeat(jnp.repeat(occupancy, size, axis=0), size, axis=1)


def plain_body(matrix, occ_matrix, batch, occ_batch, prune_mask):
    tile_size = matrix.shape[0] // occ_matrix.shape[0]
    stored_matrix = matrix * expand_tiles(occ_matrix, tile_size).astype(jnp.bfloat16)
    stored_batch = batch * expand_tiles(occ_batch, tile_size).astype(jnp.bfloat16)
    whole_batch = lax.all_gather(stored_batch, "row", axis=0, tiled=True)
    expanded = jnp.dot(
        lax.all_gather(stored_matrix, "col", axis=1, tiled=True),
        whole_batch,
        preferred_element_type=jnp.float32,
    )
    kept = expanded * prune_mask.astype(jnp.float32)
    inflated = kept * kept
    col_total = lax.psum(jnp.sum(inflated, axis=0), "row")
    order = matrix.shape[0] * lax.axis_size("row")
    return inflated / (col_total[None, :] / order + 1e-05)


def kernel(
    R, C, mat_hbm, occ_m, bat, occ_b, prune_hbm, infl_out, tot_out,
    a_buf, prune_buf, sb, bk, acc, up, down, tots,
    load_sems, s1, r1, s2, r2, f2, us, ur, ds, dr, ts, tr,
):
    rho = R // C
    rows, depth = a_buf.shape
    piece = rows // C
    tile = rows // occ_m.shape[0]
    chunk = tile
    J = rows // chunk
    r, c = lax.axis_index("row"), lax.axis_index("col")
    p, e = lax.div(r, rho), lax.rem(r, rho)

    def remote(src, dst, ssem, rsem, row, col):
        return pltpu.make_async_remote_copy(
            src_ref=src, dst_ref=dst, send_sem=ssem, recv_sem=rsem,
            device_id={"row": row, "col": col}, device_id_type=MESH,
        )

    barrier = pltpu.get_barrier_semaphore()

    def greet(row, col):
        pl.semaphore_signal(
            barrier, inc=1, device_id={"row": row, "col": col}, device_id_type=MESH
        )

    for k in range(1, C):
        greet(c * rho + e, lax.rem(c + k, C))
    for k in range(1, R):
        greet(lax.rem(r + k, R), c)

    @pl.when(c > 0)
    def _():
        greet(r, c - 1)

    @pl.when(c < C - 1)
    def _():
        greet(r, c + 1)

    load_a = pltpu.make_async_copy(mat_hbm, a_buf, load_sems.at[0])
    load_a.start()
    load_prune = pltpu.make_async_copy(prune_hbm, prune_buf, load_sems.at[1])
    load_prune.start()
    for t in range(rows // tile):
        part = pl.ds(t * tile, tile)
        sb[part, :] = bat[part, :] * occ_b[t, 0].astype(jnp.float32).astype(jnp.bfloat16)

    greeted = (
        R - 1
        + jnp.where(c > 0, 1, 0)
        + jnp.where(c < C - 1, 1, 0)
        + jnp.where(c != p, C, 0)
    )
    pl.semaphore_wait(barrier, greeted)

    def scatter(q):
        return remote(
            sb.at[pl.ds(q * piece, piece)], bk.at[e, q, c],
            s1.at[q], r1.at[c], q * rho + e, p,
        )

    for q in range(C):
        own = jnp.logical_and(p == q, c == p)

        @pl.when(own)
        def _():
            pltpu.make_async_copy(
                sb.at[pl.ds(q * piece, piece)], bk.at[e, q, c], r1.at[c]
            ).start()

        @pl.when(jnp.logical_not(own))
        def _():
            scatter(q).start()

    load_a.wait()
    for i in range(rows // tile):
        for j in range(depth // tile):
            at = (pl.ds(i * tile, tile), pl.ds(j * tile, tile))
            a_buf[at] = a_buf[at] * occ_m[i, j].astype(jnp.float32).astype(jnp.bfloat16)

    for j in range(C):
        got = bk.at[e, p, j]
        remote(got, got, s1.at[0], r1.at[j], r, c).wait_recv()

    sends = []
    for k in range(1, C):
        copy = remote(
            bk.at[e, p], bk.at[e, p], s2.at[k - 1], r2.at[e, p],
            lax.rem(p + k, C) * rho + e, c,
        )
        copy.start()
        sends.append(copy)
    for k in range(C):
        q = lax.rem(p + k, C)
        if k:
            got = bk.at[e, q]
            remote(got, got, s2.at[0], r2.at[e, q], r, c).wait_recv()
        for d in range(1, rho):
            copy = remote(
                bk.at[e, q], bk.at[e, q], f2.at[d - 1, k], r2.at[e, q],
                p * rho + lax.rem(e + d, rho), c,
            )
            copy.start()
            sends.append(copy)
    for d in range(1, rho):
        for k in range(C):
            q = lax.rem(p + k, C)
            other = lax.rem(e + d, rho)
            got = bk.at[other, q]
            remote(got, got, s2.at[0], r2.at[other, q], r, c).wait_recv()

    for i in range(C // 2 + C % 2):
        for b in sorted({C - 1 - i, i}, reverse=True):
            rhs = bk[:, :, b].reshape(depth, bk.shape[-1])
            acc[b] = jnp.dot(a_buf[...], rhs, preferred_element_type=jnp.float32)

    def up_copy(b, j):
        part = pl.ds(j * chunk, chunk)
        return remote(
            acc.at[b, part], up.at[b, part], us.at[b, j], ur.at[b, j], r, c + 1
        )

    def down_copy(b, j):
        part = pl.ds(j * chunk, chunk)
        return remote(
            acc.at[b, part], down.at[b, part], ds.at[b, j], dr.at[b, j], r, c - 1
        )

    def take(buf, sems, b, j):
        part = pl.ds(j * chunk, chunk)
        got = buf.at[b, part]
        remote(got, got, us.at[0, 0], sems.at[b, j], r, c).wait_recv()
        acc[b, part] = acc[b, part] + buf[b, part]

    for i in range(C - 1):
        for j in range(J):
            b = C - 1 - i

            @pl.when(c < b)
            def _():
                @pl.when(c > 0)
                def _():
                    take(up, ur, b, j)

                up_copy(b, j).start()

            @pl.when(c > i)
            def _():
                @pl.when(c < C - 1)
                def _():
                    take(down, dr, i, j)

                down_copy(i, j).start()

    load_prune.wait()
    for j in range(J):
        @pl.when(c > 0)
        def _():
            take(up, ur, c, j)

        @pl.when(c < C - 1)
        def _():
            take(down, dr, c, j)

    kept = acc[c] * prune_buf[...].astype(jnp.float32)
    inflated = kept * kept
    infl_out[...] = inflated
    tots[r] = jnp.broadcast_to(
        jnp.sum(inflated, axis=0, keepdims=True), tots.shape[1:]
    )
    for k in range(1, R):
        copy = remote(
            tots.at[r], tots.at[r], ts.at[k - 1], tr.at[r], lax.rem(r + k, R), c
        )
        copy.start()
        sends.append(copy)
    for k in range(1, R):
        other = lax.rem(r + k, R)
        got = tots.at[other]
        remote(got, got, ts.at[0], tr.at[other], r, c).wait_recv()
    total = tots[0]
    for k in range(1, R):
        total = total + tots[k]
    tot_out[...] = total

    for copy in sends:
        copy.wait_send()
    for q in range(C):
        @pl.when(jnp.logical_not(jnp.logical_and(p == q, c == p)))
        def _():
            scatter(q).wait_send()
    for i in range(C - 1):
        for j in range(J):
            b = C - 1 - i

            @pl.when(c < b)
            def _():
                up_copy(b, j).wait_send()

            @pl.when(c > i)
            def _():
                down_copy(i, j).wait_send()


def kernel_body(R, C, matrix, occ_matrix, batch, occ_batch, prune_mask):
    rho = R // C
    rows, depth = matrix.shape
    cols = batch.shape[1]
    J = rows // (rows // occ_matrix.shape[0])
    vmem, smem, hbm = (pl.BlockSpec(memory_space=s) for s in (pltpu.VMEM, pltpu.SMEM, pl.ANY))
    dma = pltpu.SemaphoreType.DMA
    f32, bf16 = jnp.float32, jnp.bfloat16
    inflated, total = pl.pallas_call(
        functools.partial(kernel, R, C),
        out_shape=(
            jax.ShapeDtypeStruct((rows, cols), f32),
            jax.ShapeDtypeStruct((8, cols), f32),
        ),
        in_specs=[hbm, smem, vmem, smem, hbm],
        out_specs=(vmem, vmem),
        scratch_shapes=[
            pltpu.VMEM((rows, depth), bf16),
            pltpu.VMEM((rows, cols), jnp.int32),
            pltpu.VMEM((rows, cols), bf16),
            pltpu.VMEM((rho, C, C, rows // C, cols), bf16),
            pltpu.VMEM((C, rows, cols), f32),
            pltpu.VMEM((C, rows, cols), f32),
            pltpu.VMEM((C, rows, cols), f32),
            pltpu.VMEM((R, 8, cols), f32),
            dma((2,)),
            dma((C,)),
            dma((C,)),
            dma((C - 1,)),
            dma((rho, C)),
            dma((max(rho - 1, 1), C)),
            dma((C, J)),
            dma((C, J)),
            dma((C, J)),
            dma((C, J)),
            dma((R - 1,)),
            dma((R,)),
        ],
        compiler_params=pltpu.CompilerParams(collective_id=0, has_side_effects=True),
    )(matrix, occ_matrix, batch, occ_batch, prune_mask)
    return inflated / (total[:1] / (rows * R) + 1e-05)


def body(R, C, matrix, occ_matrix, batch, occ_batch, prune_mask):
    rows = matrix.shape[0]
    fits = (
        1 < C <= 8 and R % C == 0 and R <= 16
        and rows % (16 * C) == 0 and matrix.shape[1] == rows * (R // C)
    )
    chosen = functools.partial(kernel_body, R, C) if fits else plain_body
    return chosen(matrix, occ_matrix, batch, occ_batch, prune_mask)


def solution(mesh):
    R, C = mesh.shape["row"], mesh.shape["col"]
    placed = (P("row", "col"),) * 5
    return jax.shard_map(
        functools.partial(body, R, C), mesh=mesh, in_specs=placed,
        out_specs=P("row", "col"), check_vma=False,
    )
```

```python
import functools

import jax
import jax.numpy as jnp
from jax import lax
from jax.experimental import pallas as pl
from jax.experimental.pallas import tpu as pltpu
from jax.sharding import PartitionSpec as P

MESH = pl.DeviceIdType.MESH

LOWEST = -24.0
STEPS = 2047.0
LN2 = 0.6931471805599453


def encode(x):
    safe = jnp.maximum(x, 2.0**LOWEST)
    level = jnp.minimum((jnp.log(safe) * (1.0 / LN2) - LOWEST) * STEPS, 65533.0) + 1.5
    code = jnp.where(x > 0, level.astype(jnp.int32), 0)
    return (code - 32768).astype(jnp.int16)


def decode(code):
    level = code.astype(jnp.int32) + 32767
    value = jnp.exp((level.astype(jnp.float32) * (1.0 / STEPS) + LOWEST) * LN2)
    return jnp.where(level >= 0, value, 0.0)


def expand_tiles(occupancy, size):
    return jnp.repeat(jnp.repeat(occupancy, size, axis=0), size, axis=1)


def plain_body(matrix, occ_matrix, batch, occ_batch, prune_mask):
    tile_size = matrix.shape[0] // occ_matrix.shape[0]
    stored_matrix = matrix * expand_tiles(occ_matrix, tile_size).astype(jnp.bfloat16)
    stored_batch = batch * expand_tiles(occ_batch, tile_size).astype(jnp.bfloat16)
    whole_batch = lax.all_gather(stored_batch, "row", axis=0, tiled=True)
    expanded = jnp.dot(
        lax.all_gather(stored_matrix, "col", axis=1, tiled=True),
        whole_batch,
        preferred_element_type=jnp.float32,
    )
    kept = expanded * prune_mask.astype(jnp.float32)
    inflated = kept * kept
    col_total = lax.psum(jnp.sum(inflated, axis=0), "row")
    order = matrix.shape[0] * lax.axis_size("row")
    return inflated / (col_total[None, :] / order + 1e-05)


def kernel(
    R, C, mat_hbm, occ_m, bat, occ_b, prune_hbm, infl_out, tot_out,
    a_buf, prune_buf, sb, bk, own, out_buf, in_buf, tots,
    load_sems, s1, r1, s2, r2, f2, zs, zr, ts, tr,
):
    rho = R // C
    rows, depth = a_buf.shape
    piece = rows // C
    tile = rows // occ_m.shape[0]
    r, c = lax.axis_index("row"), lax.axis_index("col")
    p, e = lax.div(r, rho), lax.rem(r, rho)

    def remote(src, dst, ssem, rsem, row, col):
        return pltpu.make_async_remote_copy(
            src_ref=src, dst_ref=dst, send_sem=ssem, recv_sem=rsem,
            device_id={"row": row, "col": col}, device_id_type=MESH,
        )

    barrier = pltpu.get_barrier_semaphore()

    def greet(row, col):
        pl.semaphore_signal(
            barrier, inc=1, device_id={"row": row, "col": col}, device_id_type=MESH
        )

    for k in range(1, C):
        greet(c * rho + e, lax.rem(c + k, C))
    for k in range(1, R):
        greet(lax.rem(r + k, R), c)

    for k in range(1, C):
        greet(r, lax.rem(c + k, C))

    load_a = pltpu.make_async_copy(mat_hbm, a_buf, load_sems.at[0])
    load_a.start()
    load_prune = pltpu.make_async_copy(prune_hbm, prune_buf, load_sems.at[1])
    load_prune.start()
    for t in range(rows // tile):
        part = pl.ds(t * tile, tile)
        sb[part, :] = bat[part, :] * occ_b[t].astype(jnp.float32).astype(jnp.bfloat16)

    greeted = R - 1 + C - 1 + jnp.where(c != p, C, 0)
    pl.semaphore_wait(barrier, greeted)

    def scatter(q):
        return remote(
            sb.at[pl.ds(q * piece, piece)], bk.at[e, q, c],
            s1.at[q], r1.at[c], q * rho + e, p,
        )

    for q in range(C):
        stays = jnp.logical_and(p == q, c == p)

        @pl.when(stays)
        def _():
            pltpu.make_async_copy(
                sb.at[pl.ds(q * piece, piece)], bk.at[e, q, c], r1.at[c]
            ).start()

        @pl.when(jnp.logical_not(stays))
        def _():
            scatter(q).start()

    load_a.wait()
    for i in range(rows // tile):
        for j in range(depth // tile):
            at = (pl.ds(i * tile, tile), pl.ds(j * tile, tile))
            a_buf[at] = a_buf[at] * occ_m[i, j].astype(jnp.float32).astype(jnp.bfloat16)

    sends = []
    order = [lax.rem(c + k, C) for k in list(range(1, C)) + [0]]

    def send(src, ssem, rsem, row):
        copy = remote(src, src, ssem, rsem, row, c)
        copy.start()
        sends.append(copy)

    def arrived(ref, rsem):
        remote(ref, ref, s1.at[0], rsem, r, c).wait_recv()

    for n, b in enumerate(order):
        mine = bk.at[e, p, b]
        arrived(mine, r1.at[b])
        for k in range(1, C):
            send(mine, s2.at[n, k], r2.at[e, p, b], lax.rem(p + k, C) * rho + e)
        for d in range(1, rho):
            send(mine, f2.at[n, d, 0], r2.at[e, p, b], p * rho + lax.rem(e + d, rho))

    for n, b in enumerate(order):
        for k in range(1, C):
            q = lax.rem(p + k, C)
            got = bk.at[e, q, b]
            arrived(got, r2.at[e, q, b])
            for d in range(1, rho):
                send(got, f2.at[n, d, k], r2.at[e, q, b], p * rho + lax.rem(e + d, rho))
        for d in range(1, rho):
            other = lax.rem(e + d, rho)
            for k in range(C):
                q = lax.rem(p + k, C)
                arrived(bk.at[other, q, b], r2.at[other, q, b])
        rhs = bk[:, :, b].reshape(depth, bk.shape[-1])
        part = jnp.dot(a_buf[...], rhs, preferred_element_type=jnp.float32)
        if n < C - 1:
            out_buf[n] = encode(part)
            copy = remote(out_buf.at[n], in_buf.at[C - 2 - n], zs.at[n], zr.at[C - 2 - n], r, b)
            copy.start()
            sends.append(copy)
        else:
            own[...] = part

    load_prune.wait()
    for n in range(C - 1):
        slot = in_buf.at[n]
        remote(slot, slot, zs.at[n], zr.at[n], r, c).wait_recv()
        own[...] = own[...] + decode(in_buf[n])

    kept = own[...] * prune_buf[...].astype(jnp.float32)
    inflated = kept * kept
    infl_out[...] = inflated
    tots[r] = jnp.broadcast_to(
        jnp.sum(inflated, axis=0, keepdims=True), tots.shape[1:]
    )
    for k in range(1, R):
        copy = remote(
            tots.at[r], tots.at[r], ts.at[k - 1], tr.at[r], lax.rem(r + k, R), c
        )
        copy.start()
        sends.append(copy)
    for k in range(1, R):
        other = lax.rem(r + k, R)
        got = tots.at[other]
        remote(got, got, ts.at[0], tr.at[other], r, c).wait_recv()
    total = tots[0]
    for k in range(1, R):
        total = total + tots[k]
    tot_out[...] = total / (rows * R) + 1e-05

    for copy in sends:
        copy.wait_send()
    for q in range(C):
        @pl.when(jnp.logical_not(jnp.logical_and(p == q, c == p)))
        def _():
            scatter(q).wait_send()


def kernel_body(R, C, matrix, occ_matrix, batch, occ_batch, prune_mask):
    rho = R // C
    rows, depth = matrix.shape
    cols = batch.shape[1]
    vmem, smem, hbm = (pl.BlockSpec(memory_space=s) for s in (pltpu.VMEM, pltpu.SMEM, pl.ANY))
    dma = pltpu.SemaphoreType.DMA
    f32, bf16 = jnp.float32, jnp.bfloat16
    inflated, total = pl.pallas_call(
        functools.partial(kernel, R, C),
        out_shape=(
            jax.ShapeDtypeStruct((rows, cols), f32),
            jax.ShapeDtypeStruct((1, cols), f32),
        ),
        in_specs=[hbm, smem, vmem, smem, hbm],
        out_specs=(vmem, vmem),
        scratch_shapes=[
            pltpu.VMEM((rows, depth), bf16),
            pltpu.VMEM((rows, cols), jnp.int32),
            pltpu.VMEM((rows, cols), bf16),
            pltpu.VMEM((rho, C, C, rows // C, cols), bf16),
            pltpu.VMEM((rows, cols), f32),
            pltpu.VMEM((C - 1, rows, cols), jnp.int16),
            pltpu.VMEM((C - 1, rows, cols), jnp.int16),
            pltpu.VMEM((R, 1, cols), f32),
            dma((2,)),
            dma((C,)),
            dma((C,)),
            dma((C, C)),
            dma((rho, C, C)),
            dma((C, rho, C)),
            dma((C - 1,)),
            dma((C - 1,)),
            dma((R - 1,)),
            dma((R,)),
        ],
        compiler_params=pltpu.CompilerParams(collective_id=0, has_side_effects=True),
    )(matrix, occ_matrix, batch, occ_batch[:, 0], prune_mask)
    return inflated / total


def body(R, C, matrix, occ_matrix, batch, occ_batch, prune_mask):
    rows = matrix.shape[0]
    fits = (
        1 < C <= 8 and R % C == 0 and R <= 16
        and rows % (16 * C) == 0 and matrix.shape[1] == rows * (R // C)
    )
    chosen = functools.partial(kernel_body, R, C) if fits else plain_body
    return chosen(matrix, occ_matrix, batch, occ_batch, prune_mask)


def solution(mesh):
    R, C = mesh.shape["row"], mesh.shape["col"]
    placed = (P("row", "col"),) * 5
    return jax.shard_map(
        functools.partial(body, R, C), mesh=mesh, in_specs=placed,
        out_specs=P("row", "col"), check_vma=False,
    )
```

```python
import functools

import jax
import jax.numpy as jnp
from jax import lax
from jax.experimental import pallas as pl
from jax.experimental.pallas import tpu as pltpu
from jax.sharding import PartitionSpec as P

MESH = pl.DeviceIdType.MESH

LOWEST = -24.0
STEPS = 2047.0
LN2 = 0.6931471805599453


def encode(x):
    safe = jnp.maximum(x, 2.0**LOWEST)
    level = jnp.minimum((jnp.log(safe) * (1.0 / LN2) - LOWEST) * STEPS, 65533.0) + 1.5
    code = jnp.where(x > 0, level.astype(jnp.int32), 0)
    return (code - 32768).astype(jnp.int16)


def decode(code):
    level = code.astype(jnp.int32) + 32767
    value = jnp.exp((level.astype(jnp.float32) * (1.0 / STEPS) + LOWEST) * LN2)
    return jnp.where(level >= 0, value, 0.0)


def expand_tiles(occupancy, size):
    return jnp.repeat(jnp.repeat(occupancy, size, axis=0), size, axis=1)


def plain_body(matrix, occ_matrix, batch, occ_batch, prune_mask):
    tile_size = matrix.shape[0] // occ_matrix.shape[0]
    stored_matrix = matrix * expand_tiles(occ_matrix, tile_size).astype(jnp.bfloat16)
    stored_batch = batch * expand_tiles(occ_batch, tile_size).astype(jnp.bfloat16)
    whole_batch = lax.all_gather(stored_batch, "row", axis=0, tiled=True)
    expanded = jnp.dot(
        lax.all_gather(stored_matrix, "col", axis=1, tiled=True),
        whole_batch,
        preferred_element_type=jnp.float32,
    )
    kept = expanded * prune_mask.astype(jnp.float32)
    inflated = kept * kept
    col_total = lax.psum(jnp.sum(inflated, axis=0), "row")
    order = matrix.shape[0] * lax.axis_size("row")
    return inflated / (col_total[None, :] / order + 1e-05)


def kernel(
    R, C, mat_hbm, occ_m, bat, occ_b, prune_hbm, infl_out, tot_out,
    a_buf, prune_buf, sb, bk, own, out_buf, in_buf, tots,
    load_sems, s1, r1, s2, r2, f2, zs, zr, ts, tr,
):
    rho = R // C
    rows, depth = a_buf.shape
    piece = rows // C
    tile = rows // occ_m.shape[0]
    r, c = lax.axis_index("row"), lax.axis_index("col")
    p, e = lax.div(r, rho), lax.rem(r, rho)

    def remote(src, dst, ssem, rsem, row, col):
        return pltpu.make_async_remote_copy(
            src_ref=src, dst_ref=dst, send_sem=ssem, recv_sem=rsem,
            device_id={"row": row, "col": col}, device_id_type=MESH,
        )

    barrier = pltpu.get_barrier_semaphore()

    def greet(row, col):
        pl.semaphore_signal(
            barrier, inc=1, device_id={"row": row, "col": col}, device_id_type=MESH
        )

    for k in range(1, C):
        greet(c * rho + e, lax.rem(c + k, C))
    for k in range(1, R):
        greet(lax.rem(r + k, R), c)

    for k in range(1, C):
        greet(r, lax.rem(c + k, C))

    load_a = pltpu.make_async_copy(mat_hbm, a_buf, load_sems.at[0])
    load_a.start()
    load_prune = pltpu.make_async_copy(prune_hbm, prune_buf, load_sems.at[1])
    load_prune.start()
    for t in range(rows // tile):
        part = pl.ds(t * tile, tile)
        sb[part, :] = bat[part, :] * occ_b[t].astype(jnp.float32).astype(jnp.bfloat16)

    greeted = R - 1 + C - 1 + jnp.where(c != p, C, 0)
    pl.semaphore_wait(barrier, greeted)

    def scatter(q):
        return remote(
            sb.at[pl.ds(q * piece, piece)], bk.at[e, q, c],
            s1.at[q], r1.at[c], q * rho + e, p,
        )

    for q in range(C):
        stays = jnp.logical_and(p == q, c == p)

        @pl.when(stays)
        def _():
            pltpu.make_async_copy(
                sb.at[pl.ds(q * piece, piece)], bk.at[e, q, c], r1.at[c]
            ).start()

        @pl.when(jnp.logical_not(stays))
        def _():
            scatter(q).start()

    load_a.wait()
    for i in range(rows // tile):
        for j in range(depth // tile):
            at = (pl.ds(i * tile, tile), pl.ds(j * tile, tile))
            a_buf[at] = a_buf[at] * occ_m[i, j].astype(jnp.float32).astype(jnp.bfloat16)

    sends = []
    reach = jnp.minimum(c, C - 1 - c)

    def nearest(n):
        near = c - (n + 1) // 2 if n % 2 else c + n // 2
        far = jnp.where(c < C - 1 - c, n, C - 1 - n)
        return jnp.where(n <= 2 * reach, near, far)

    order = [nearest(n) for n in list(range(C - 1, 0, -1)) + [0]]

    def send(src, ssem, rsem, row):
        copy = remote(src, src, ssem, rsem, row, c)
        copy.start()
        sends.append(copy)

    def arrived(ref, rsem):
        remote(ref, ref, s1.at[0], rsem, r, c).wait_recv()

    for n, b in enumerate(order):
        mine = bk.at[e, p, b]
        arrived(mine, r1.at[b])
        for k in range(1, C):
            send(mine, s2.at[n, k], r2.at[e, p, b], lax.rem(p + k, C) * rho + e)
        for d in range(1, rho):
            send(mine, f2.at[n, d, 0], r2.at[e, p, b], p * rho + lax.rem(e + d, rho))

    for n, b in enumerate(order):
        for k in range(1, C):
            q = lax.rem(p + k, C)
            got = bk.at[e, q, b]
            arrived(got, r2.at[e, q, b])
            for d in range(1, rho):
                send(got, f2.at[n, d, k], r2.at[e, q, b], p * rho + lax.rem(e + d, rho))
        for d in range(1, rho):
            other = lax.rem(e + d, rho)
            for k in range(C):
                q = lax.rem(p + k, C)
                arrived(bk.at[other, q, b], r2.at[other, q, b])
        rhs = bk[:, :, b].reshape(depth, bk.shape[-1])
        part = jnp.dot(a_buf[...], rhs, preferred_element_type=jnp.float32)
        if n < C - 1:
            out_buf[n] = encode(part)
            copy = remote(out_buf.at[n], in_buf.at[c], zs.at[n], zr.at[c], r, b)
            copy.start()
            sends.append(copy)
        else:
            own[...] = part

    load_prune.wait()
    for n in range(C - 1):
        other = order[C - 2 - n]
        arrived(in_buf.at[other], zr.at[other])
        own[...] = own[...] + decode(in_buf[other])

    kept = own[...] * prune_buf[...].astype(jnp.float32)
    inflated = kept * kept
    tots[r] = jnp.broadcast_to(
        jnp.sum(inflated, axis=0, keepdims=True), tots.shape[1:]
    )
    for k in range(1, R):
        copy = remote(
            tots.at[r], tots.at[r], ts.at[k - 1], tr.at[r], lax.rem(r + k, R), c
        )
        copy.start()
        sends.append(copy)
    for k in range(1, R):
        other = lax.rem(r + k, R)
        got = tots.at[other]
        remote(got, got, ts.at[0], tr.at[other], r, c).wait_recv()
    total = tots[0]
    for k in range(1, R):
        total = total + tots[k]
    infl_out[...] = inflated / (total / (rows * R) + 1e-05)
    tot_out[...] = total

    for copy in sends:
        copy.wait_send()
    for q in range(C):
        @pl.when(jnp.logical_not(jnp.logical_and(p == q, c == p)))
        def _():
            scatter(q).wait_send()


def kernel_body(R, C, matrix, occ_matrix, batch, occ_batch, prune_mask):
    rho = R // C
    rows, depth = matrix.shape
    cols = batch.shape[1]
    vmem, smem, hbm = (pl.BlockSpec(memory_space=s) for s in (pltpu.VMEM, pltpu.SMEM, pl.ANY))
    dma = pltpu.SemaphoreType.DMA
    f32, bf16 = jnp.float32, jnp.bfloat16
    inflated, total = pl.pallas_call(
        functools.partial(kernel, R, C),
        out_shape=(
            jax.ShapeDtypeStruct((rows, cols), f32),
            jax.ShapeDtypeStruct((1, cols), f32),
        ),
        in_specs=[hbm, smem, vmem, smem, hbm],
        out_specs=(vmem, vmem),
        scratch_shapes=[
            pltpu.VMEM((rows, depth), bf16),
            pltpu.VMEM((rows, cols), jnp.int32),
            pltpu.VMEM((rows, cols), bf16),
            pltpu.VMEM((rho, C, C, rows // C, cols), bf16),
            pltpu.VMEM((rows, cols), f32),
            pltpu.VMEM((C - 1, rows, cols), jnp.int16),
            pltpu.VMEM((C, rows, cols), jnp.int16),
            pltpu.VMEM((R, 1, cols), f32),
            dma((2,)),
            dma((C,)),
            dma((C,)),
            dma((C, C)),
            dma((rho, C, C)),
            dma((C, rho, C)),
            dma((C - 1,)),
            dma((C,)),
            dma((R - 1,)),
            dma((R,)),
        ],
        compiler_params=pltpu.CompilerParams(collective_id=0, has_side_effects=True),
    )(matrix, occ_matrix, batch, occ_batch[:, 0], prune_mask)
    return inflated


def body(R, C, matrix, occ_matrix, batch, occ_batch, prune_mask):
    rows = matrix.shape[0]
    fits = (
        1 < C <= 8 and R % C == 0 and R <= 16
        and rows % (16 * C) == 0 and matrix.shape[1] == rows * (R // C)
    )
    chosen = functools.partial(kernel_body, R, C) if fits else plain_body
    return chosen(matrix, occ_matrix, batch, occ_batch, prune_mask)


def solution(mesh):
    R, C = mesh.shape["row"], mesh.shape["col"]
    placed = (P("row", "col"),) * 5
    return jax.shard_map(
        functools.partial(body, R, C), mesh=mesh, in_specs=placed,
        out_specs=P("row", "col"), check_vma=False,
    )
```
